32 devices in a mesh: ctx: 16 (over z, y, x), fsdp: 2 (over core).
Axes of the slice: x: 2, y: 2, z: 4, core: 2. Of those that a mesh axis runs over, the one named last changes fastest.
Arguments:
- tokens: bfloat16 [2, 2048, 768], P('fsdp', 'ctx'), may hold values from -6 to 6
- cluster_ids: int32 [2, 2048, 12], P('fsdp', 'ctx'), may hold values from 0 to 15, as said below
- qkv_weight: bfloat16 [768, 2304], P('fsdp'), may hold values from -0.21875 to 0.21875
- out_weight: bfloat16 [768, 768], P('fsdp'), may hold values from -2 to 2
- up_weight: bfloat16 [768, 3072], P('fsdp'), may hold values from -0.21875 to 0.21875
- down_weight: bfloat16 [3072, 768], P('fsdp'), may hold values from -0.109375 to 0.109375
- query_bias: float32 [768], P('fsdp'), may hold values from -1 to 1
- value_bias: float32 [768], P('fsdp'), may hold values from -1 to 1
- out_bias: float32 [768], P('fsdp'), may hold values from -1 to 1
- up_bias: float32 [3072], P('fsdp'), may hold values from -1 to 1
- down_bias: float32 [768], P('fsdp'), may hold values from -1 to 1
- first_gain: float32 [768], P('fsdp'), may hold values from 0.25 to 1.75
- first_shift: float32 [768], P('fsdp'), may hold values from -1 to 1
- second_gain: float32 [768], P('fsdp'), may hold values from 0.25 to 1.75
- second_shift: float32 [768], P('fsdp'), may hold values from -1 to 1
- cotangent: bfloat16 [2, 2048, 768], P('fsdp', 'ctx'), may hold values from -6 to 6
Outputs:
- layer_out: bfloat16 [2, 2048, 768], P('fsdp', 'ctx')
- input_grad: bfloat16 [2, 2048, 768], P('fsdp', 'ctx')
- qkv_weight_grad: float32 [768, 2304], P('fsdp')
- out_weight_grad: float32 [768, 768], P('fsdp')
- up_weight_grad: float32 [768, 3072], P('fsdp')
- down_weight_grad: float32 [3072, 768], P('fsdp')
- query_bias_grad: float32 [768], P('fsdp')
- value_bias_grad: float32 [768], P('fsdp')
- out_bias_grad: float32 [768], P('fsdp')
- up_bias_grad: float32 [3072], P('fsdp')
- down_bias_grad: float32 [768], P('fsdp')
- first_gain_grad: float32 [768], P('fsdp')
- first_shift_grad: float32 [768], P('fsdp')
- second_gain_grad: float32 [768], P('fsdp')
- second_shift_grad: float32 [768], P('fsdp')
The draws below stay inside these ranges and needn't reach their ends.
Inputs may be any that keep to these rules, and one draw needn't show every extreme that they name: `cluster_ids`: for each sequence and head, every cluster id is held by exactly 128 tokens of that sequence.
All inputs are finite; a program needn't handle non-finite values.
Results may differ from the reference program's by a relative error of at most 0.04.
Values may be sent and summed in bfloat16 or wider, within the bound.
No kernel may reach another device: no remote copies, remote signals or barrier semaphores. Data moves between devices by JAX's collectives and lax.ppermute only.
A program may use at most 192 MiB of HBM per device.

```python
import math
import jax
import jax.numpy as jnp
from jax import lax

D = 768
HEADS = 12
HEAD_DIM = 64
FF = 3072
BLOCK = 256
CLUSTER = 128
LEN = 2048
SEQS = 2


def draw_cluster_ids(key, part):
    streams = jax.random.split(key, SEQS * HEADS)
    orders = jax.vmap(lambda stream: jax.random.permutation(stream, LEN))(streams)
    labels = (orders // CLUSTER).astype(jnp.int32).reshape(SEQS, HEADS, LEN)
    return jnp.transpose(labels, (0, 2, 1))


def level_of(rng, shape, shards, least, top_value):
    factor_of, own = 1.0, jax.random.fold_in(rng, 6)
    for position, blocks in shards:
        draws = jnp.exp(jax.random.uniform(jax.random.fold_in(own, position), (blocks,), jnp.float32, least / len(shards), top_value / len(shards)))
        factor_of = factor_of * jnp.repeat(draws, shape[position] // blocks).reshape([-1 if axis == position else 1 for axis in range(len(shape))])
    return factor_of


def centred(own_key, dims, scale, most, cuts=(), kind=jnp.bfloat16):
    array = scale * jax.random.normal(own_key, dims, jnp.float32)
    if cuts:
        array = array * level_of(own_key, dims, cuts, -0.22, 0.18)
    return jnp.clip(array, -most, most).astype(kind)


def setup_inputs(seed: int = 0) -> dict:
    key_of = jax.random.split(jax.random.key(seed), 17)
    return {
        "tokens": centred(key_of[0], (SEQS, LEN, D), 1.0, 6.0, ((0, 2), (1, 16))),
        "cluster_ids": draw_cluster_ids(jax.random.fold_in(key_of[16], 71), 0),
        "qkv_weight": centred(key_of[2], (D, 3 * D), D ** -0.5, 0.21875, ((0, 2),)),
        "out_weight": centred(key_of[3], (D, D), (max(D // 96, 2)) ** -0.5, 2.0, ((0, 2),)),
        "up_weight": centred(key_of[4], (D, FF), D ** -0.5, 0.21875, ((0, 2),)),
        "down_weight": centred(key_of[5], (FF, D), FF ** -0.5, 0.109375, ((0, 2),)),
        "query_bias": centred(key_of[6], (D,), 0.2, 1.0, ((0, 2),), jnp.float32),
        "value_bias": centred(key_of[7], (D,), 0.2, 1.0, ((0, 2),), jnp.float32),
        "out_bias": centred(key_of[8], (D,), 0.2, 1.0, ((0, 2),), jnp.float32),
        "up_bias": centred(key_of[9], (FF,), 0.2, 1.0, ((0, 2),), jnp.float32),
        "down_bias": centred(key_of[10], (D,), 0.2, 1.0, ((0, 2),), jnp.float32),
        "first_gain": jnp.clip(1.0 + 0.15 * jax.random.normal(key_of[11], (D,), jnp.float32), 0.25, 1.75),
        "first_shift": centred(key_of[12], (D,), 0.2, 1.0, ((0, 2),), jnp.float32),
        "second_gain": jnp.clip(1.0 + 0.15 * jax.random.normal(key_of[13], (D,), jnp.float32), 0.25, 1.75),
        "second_shift": centred(key_of[14], (D,), 0.2, 1.0, ((0, 2),), jnp.float32),
        "cotangent": centred(key_of[15], (SEQS, LEN, D), 1.0, 6.0, ((0, 2), (1, 16))),
    }


NEG = -1e+30
EPS = 1e-05
HIGH = lax.Precision.HIGHEST

@jax.custom_vjp
def low(v):
    return lax.optimization_barrier(v.astype(jnp.bfloat16)).astype(jnp.float32)

@jax.custom_vjp
def low_back(v):
    return v

def low_keep(v):
    return (low(v), None)

def low_pass(kept, grad):
    return (grad,)

def back_keep(v):
    return (v, None)

def back_low(kept, grad):
    return (low(grad),)
low.defvjp(low_keep, low_pass)
low_back.defvjp(back_keep, back_low)

def layer_norm(resid, gain, shift):
    center = lax.optimization_barrier(jnp.mean(resid, axis=-1, keepdims=True))
    centered = resid - center
    spread = lax.optimization_barrier(jnp.mean(centered * centered, axis=-1, keepdims=True))
    return centered * lax.rsqrt(spread + EPS) * gain + shift

def attention(queries, keys, values, ids):
    length = queries.shape[0]
    scale = 1.0 / math.sqrt(HEAD_DIM)
    query3 = queries.reshape(length, HEADS, HEAD_DIM)
    key3 = keys.reshape(length, HEADS, HEAD_DIM)
    value3 = values.reshape(length, HEADS, HEAD_DIM)
    key_block = lax.iota(jnp.int32, length) // BLOCK
    key_ids = jnp.transpose(ids)

    def one_block(index):
        start = (index * BLOCK).astype(jnp.int32)
        query_rows = lax.dynamic_slice_in_dim(query3, start, BLOCK, 0)
        query_ids = lax.dynamic_slice_in_dim(ids, start, BLOCK, 0)
        query_block = (start + lax.iota(jnp.int32, BLOCK)) // BLOCK
        same = (query_block[:, None] == key_block[None, :])[:, None, :]
        earlier = (key_block[None, :] < query_block[:, None])[:, None, :]
        match = query_ids[:, :, None] == key_ids[None, :, :]
        allowed = same | earlier & match
        scores = low_back(jnp.einsum('qhd,khd->qhk', query_rows, key3, precision=HIGH) * scale)
        masked = jnp.where(allowed, scores, NEG)
        total = jax.nn.logsumexp(masked, axis=-1, keepdims=True)
        probs = low(jnp.exp(masked - total))
        return jnp.einsum('qhk,khd->qhd', probs, value3, precision=HIGH)
    blocks = lax.map(jax.checkpoint(one_block), jnp.arange(length // BLOCK, dtype=jnp.int32))
    return blocks.reshape(length, HEADS * HEAD_DIM)

def layer(inputs, ids, params):
    qkv_weight, out_weight, up_weight, down_weight, query_bias, value_bias, out_bias, up_bias, down_bias, first_gain, first_shift, second_gain, second_shift = params
    width = inputs.shape[1]
    projected = jnp.dot(inputs, qkv_weight, precision=HIGH)
    queries = low(low_back(projected[:, :width] + query_bias))
    keys = low(low_back(projected[:, width:2 * width]))
    values = low(low_back(projected[:, 2 * width:] + value_bias))
    attended = low(low_back(attention(queries, keys, values, ids)))
    branch = low_back(jnp.dot(attended, out_weight, precision=HIGH)) + out_bias
    hidden = layer_norm(inputs + branch, first_gain, first_shift)
    pre_act = low_back(jnp.dot(low(hidden), up_weight, precision=HIGH)) + up_bias
    activ = low(jax.nn.gelu(pre_act, approximate=False))
    ffn = low_back(jnp.dot(activ, down_weight, precision=HIGH)) + down_bias
    return layer_norm(hidden + ffn, second_gain, second_shift)

def reference(tokens, cluster_ids, qkv_weight, out_weight, up_weight, down_weight, query_bias, value_bias, out_bias, up_bias, down_bias, first_gain, first_shift, second_gain, second_shift, cotangent):
    params = tuple((item.astype(jnp.float32) for item in (qkv_weight, out_weight, up_weight, down_weight, query_bias, value_bias, out_bias, up_bias, down_bias, first_gain, first_shift, second_gain, second_shift)))

    def forward(inputs, weights):

        def per_sequence(pair):
            return layer(pair[0], pair[1], weights)
        return lax.map(per_sequence, (inputs, cluster_ids))
    result, pull = jax.vjp(forward, tokens.astype(jnp.float32), params)
    grad_inputs, grads = pull(cotangent.astype(jnp.float32))
    return (result.astype(jnp.bfloat16), grad_inputs.astype(jnp.bfloat16), grads[0], grads[1], grads[2], grads[3], grads[4], grads[5], grads[6], grads[7], grads[8], grads[9], grads[10], grads[11], grads[12])
```

```python
import functools
import math

import jax
import jax.numpy as jnp
from jax import lax
from jax.experimental import pallas as pl
from jax.experimental.pallas import tpu as pltpu
from jax.sharding import PartitionSpec as P

HEADS = 12
HEAD_DIM = 64
BLOCK = 256
CLUSTER = 128
EPS = 1e-05
FEAT = 128
FAR = 2.0**100
F32 = jnp.float32
BF = jnp.bfloat16


def dot(a,b): return jnp.dot(a,b,preferred_element_type=F32)
def dot_nt(a,b): return lax.dot_general(a,b,(((1,),(1,)),((),())),preferred_element_type=F32)

def fwd_body(x_ref, o_ref, full_ref, lse_ref, qf_ref, kf_ref, vt_ref):
    pieces, rows_in, rows = x_ref.shape
    length = pieces*rows
    clusters = length // 128
    nb = length // BLOCK
    def build(j, _):
        at = pl.ds(pl.multiple_of(j*rows, rows), rows)
        q = x_ref[j, 0:64, :]; k = x_ref[j, 64:128, :]; v = x_ref[j,128:192,:]
        ids = x_ref[j, 192:200, :].astype(F32)[0:1, :]
        row = lax.broadcasted_iota(jnp.int32, (FEAT-HEAD_DIM, rows), 0).astype(F32)
        same = row == ids
        qf_ref[:, at] = jnp.concatenate([q, same.astype(F32).astype(BF)], axis=0)
        far = jnp.where(same, 0.0, -FAR).astype(BF)
        kf_ref[at, :] = jnp.concatenate([k, far], axis=0).T
        vt_ref[:, at] = v
        return 0
    lax.fori_loop(0, pieces, build, 0)
    def qstep(qb, _):
        qat = pl.ds(pl.multiple_of(qb*BLOCK, BLOCK), BLOCK)
        q = qf_ref[:, qat]
        s = dot(kf_ref[qat, 0:HEAD_DIM], q[0:HEAD_DIM])
        m = jnp.max(s, axis=0, keepdims=True)
        p = jnp.exp(s-m)
        l = jnp.sum(p, axis=0, keepdims=True)
        acc = dot(vt_ref[:, qat], p.astype(BF))
        def kstep(kb, c):
            m,l,acc = c
            kat = pl.ds(pl.multiple_of(kb*BLOCK, BLOCK), BLOCK)
            s = dot(kf_ref[kat,:], q)
            m2 = jnp.maximum(m, jnp.max(s,axis=0,keepdims=True))
            a = jnp.exp(m-m2); p = jnp.exp(s-m2)
            l = l*a + jnp.sum(p,axis=0,keepdims=True)
            acc = acc*a + dot(vt_ref[:,kat], p.astype(BF))
            return m2,l,acc
        m,l,acc = lax.fori_loop(0, qb, kstep, (m,l,acc))
        o = acc / l
        full_ref[:, qat] = o
        lse_ref[:, qat] = m + jnp.log(l)
        ob = o.astype(BF)
        for t in range(BLOCK//rows):
            o_ref[qb*(BLOCK//rows)+t] = ob[:, t*rows:(t+1)*rows]
        return 0
    lax.fori_loop(0, nb, qstep, 0)

def attn_fwd(x):
    pieces, _, rows = x.shape; length=pieces*rows
    outs = (jax.ShapeDtypeStruct((pieces,HEAD_DIM,rows),BF), jax.ShapeDtypeStruct((HEAD_DIM,length),F32),
            jax.ShapeDtypeStruct((1,length),F32), jax.ShapeDtypeStruct((FEAT,length),BF), jax.ShapeDtypeStruct((length,FEAT),BF), jax.ShapeDtypeStruct((HEAD_DIM,length),BF))
    return pl.pallas_call(fwd_body, out_shape=outs,
        in_specs=[pl.BlockSpec(memory_space=pltpu.VMEM)], out_specs=tuple(pl.BlockSpec(memory_space=pltpu.VMEM) for _ in outs),
        compiler_params=pltpu.CompilerParams(vmem_limit_bytes=48<<20), name="attention_forward")(x)

def bwd_body(x_ref, g_ref, full_ref, lse_ref, qf_ref, kf_ref, vt_ref, out_ref, gt_ref, delta_ref, v_ref, kt_ref, dk_ref, dv_ref):
    pieces, rows_in, rows = x_ref.shape
    length = pieces*rows
    nb = length // BLOCK
    def build(j, _):
        at = pl.ds(pl.multiple_of(j*rows, rows), rows)
        g = g_ref[j]
        gt_ref[:, at] = g
        delta_ref[:, at] = jnp.sum(g.astype(F32)*full_ref[:, at], axis=0, keepdims=True)
        v_ref[at,:] = x_ref[j,128:192,:].T
        kt_ref[:, at] = x_ref[j,64:128,:]
        return 0
    lax.fori_loop(0, pieces, build, 0)
    def block(kat, qat, feats, first):
        q = qf_ref[0:feats, qat]
        lse = lse_ref[:, qat]
        g = gt_ref[:, qat]
        s = dot(kf_ref[kat,0:feats], q)
        p = jnp.exp(s - lse)
        dp = dot(v_ref[kat,:], g)
        ds = (p*(dp - delta_ref[:, qat])).astype(BF)
        dv = dot_nt(g, p.astype(BF))
        dk = dot_nt(q[0:HEAD_DIM], ds)
        if first:
            dv_ref[:,kat] = dv; dk_ref[:,kat] = dk
        else:
            dv_ref[:,kat] += dv; dk_ref[:,kat] += dk
        return dot(kt_ref[:,kat], ds)
    def qstep(qb, _):
        qat = pl.ds(pl.multiple_of(qb*BLOCK, BLOCK), BLOCK)
        dq = block(qat, qat, HEAD_DIM, True)
        def kstep(kb, dq):
            kat = pl.ds(pl.multiple_of(kb*BLOCK, BLOCK), BLOCK)
            return dq + block(kat, qat, FEAT, False)
        dq = lax.fori_loop(0, qb, kstep, dq)
        dqb = (dq*(1.0/math.sqrt(HEAD_DIM))).astype(BF)
        for t in range(BLOCK//rows):
            out_ref[qb*(BLOCK//rows)+t, 0:64, :] = dqb[:, t*rows:(t+1)*rows]
        return 0
    lax.fori_loop(0, nb, qstep, 0)
    def finish(j, _):
        at = pl.ds(pl.multiple_of(j*rows, rows), rows)
        out_ref[j, 64:128, :] = dk_ref[:, at].astype(BF)
        out_ref[j, 128:192, :] = dv_ref[:, at].astype(BF)
        return 0
    lax.fori_loop(0, pieces, finish, 0)

def attn_bwd(x, g, full, lse, qf, kf, vt):
    pieces, _, rows = x.shape; length=pieces*rows
    return pl.pallas_call(bwd_body, out_shape=jax.ShapeDtypeStruct((pieces,3*HEAD_DIM,rows),BF),
        in_specs=[pl.BlockSpec(memory_space=pltpu.VMEM)]*7, out_specs=pl.BlockSpec(memory_space=pltpu.VMEM),
        scratch_shapes=[pltpu.VMEM((HEAD_DIM,length),BF), pltpu.VMEM((1,length),F32), pltpu.VMEM((length,HEAD_DIM),BF), pltpu.VMEM((HEAD_DIM,length),BF),
            pltpu.VMEM((HEAD_DIM,length),F32), pltpu.VMEM((HEAD_DIM,length),F32)],
        compiler_params=pltpu.CompilerParams(vmem_limit_bytes=48<<20), name="attention_backward")(x,g,full,lse,qf,kf,vt)


def layer_norm(resid, gain, shift):
    center = jnp.mean(resid, axis=-1, keepdims=True)
    centered = resid - center
    spread = jnp.mean(centered * centered, axis=-1, keepdims=True)
    return centered * lax.rsqrt(spread + EPS) * gain + shift


def gelu_exact(value):
    return jax.nn.gelu(value, approximate=False)


def contract(left, right, left_dim, right_dim):
    return lax.dot_general(
        left, right, (((left_dim,), (right_dim,)), ((), ())), preferred_element_type=F32
    )


def swap(value):
    return lax.ppermute(value, "fsdp", [(0, 1), (1, 0)])


def half_of(value, index, axis):
    size = value.shape[axis] // 2
    return lax.dynamic_slice_in_dim(value, index * size, size, axis)


def exchange(value, bit, count):
    return lax.ppermute(value, "ctx", [(i, i ^ (1 << bit)) for i in range(count)])


def split_axis(shape):
    if (shape[0] // 2) % 16 == 0:
        return 0
    if (shape[1] // 2) % 128 == 0:
        return 1
    return 0


def reduce_scatter(value, order, count, index):
    axes = []
    for bit in order:
        axis = split_axis(value.shape)
        axes.append(axis)
        mine = (index >> bit) & 1
        arrived = exchange(half_of(value, 1 - mine, axis), bit, count)
        value = (half_of(value, mine, axis).astype(F32) + arrived.astype(F32)).astype(BF)
    return value, axes


def gather_back(value, order, axes, count, index):
    for bit, axis in zip(reversed(order), reversed(axes)):
        arrived = exchange(value, bit, count)
        mine = (index >> bit) & 1
        value = jnp.where(
            mine == 0,
            jnp.concatenate([value, arrived], axis),
            jnp.concatenate([arrived, value], axis),
        )
    return value


def sum_over_tokens(value, cuts, orders, count, index):
    pieces = []
    start = 0
    for size, order in zip(cuts, orders):
        part, axes = reduce_scatter(value[:, start : start + size], order, count, index)
        pieces.append(gather_back(part, order, axes, count, index))
        start += size
    return jnp.concatenate(pieces, 1).astype(F32)


def per_device(
    count,
    tokens,
    cluster_ids,
    qkv_weight,
    out_weight,
    up_weight,
    down_weight,
    query_bias,
    value_bias,
    out_bias,
    up_bias,
    down_bias,
    first_gain,
    first_shift,
    second_gain,
    second_shift,
    cotangent,
):
    side = lax.axis_index("fsdp")
    place = lax.axis_index("ctx")
    other = 1 - side
    vectors = (
        query_bias,
        value_bias,
        out_bias,
        up_bias,
        down_bias,
        first_gain,
        first_shift,
        second_gain,
        second_shift,
    )
    sizes = [item.shape[0] for item in vectors]
    starts = [sum(sizes[:i]) for i in range(len(sizes) + 1)]
    qkv_other = swap(qkv_weight)
    packed = jnp.concatenate(vectors)
    packed_other = swap(packed)
    out_other, up_other, down_other = swap(out_weight), swap(up_weight), swap(down_weight)
    low_half = jnp.where(side == 0, packed, packed_other)
    high_half = jnp.where(side == 0, packed_other, packed)

    def whole(i):
        return jnp.concatenate(
            [low_half[starts[i] : starts[i + 1]], high_half[starts[i] : starts[i + 1]]]
        )

    bias_q, bias_v, bias_out, bias_up, bias_down, gain_one, shift_one, gain_two, shift_two = (
        whole(i) for i in range(9)
    )
    inputs = tokens[0]
    rows, width = inputs.shape
    slots = -(-HEADS // count) * count
    per = slots // count
    scale = 1.0 / math.sqrt(HEAD_DIM)

    in_mine, in_other = half_of(inputs, side, 1), half_of(inputs, other, 1)
    projected = contract(qkv_weight, in_mine, 0, 1) + contract(qkv_other, in_other, 0, 1)
    queries = ((projected[:width] + bias_q[:, None]) * scale).astype(BF)
    keys = projected[width : 2 * width].astype(BF)
    values = (projected[2 * width :] + bias_v[:, None]).astype(BF)
    ids = jnp.transpose(cluster_ids[0]).astype(BF)
    chunks = jnp.concatenate(
        [
            queries.reshape(HEADS, HEAD_DIM, rows),
            keys.reshape(HEADS, HEAD_DIM, rows),
            values.reshape(HEADS, HEAD_DIM, rows),
            jnp.broadcast_to(ids[:, None, :], (HEADS, 8, rows)),
        ],
        axis=1,
    )
    chunks = jnp.pad(chunks, ((0, slots - HEADS), (0, 0), (0, 0)))

    def to_heads(value):
        return lax.all_to_all(
            value.reshape(count, per, *value.shape[1:]), "ctx", 0, 0, tiled=False
        )

    def to_tokens(value):
        arrived = lax.all_to_all(value, "ctx", 0, 0, tiled=False)
        return arrived.reshape(slots, *arrived.shape[2:])[:HEADS]

    gathered = to_heads(chunks)
    kept = [attn_fwd(gathered[:, i]) for i in range(per)]
    attended = to_tokens(jnp.stack([item[0] for item in kept], 1)).reshape(width, rows)
    att_mine, att_other = half_of(attended, side, 0), half_of(attended, other, 0)
    branch = contract(att_mine, out_weight, 0, 0) + contract(att_other, out_other, 0, 0)
    resid_one = inputs.astype(F32) + branch + bias_out
    hidden = layer_norm(resid_one, gain_one, shift_one)
    hidden_low = hidden.astype(BF)
    hid_mine, hid_other = half_of(hidden_low, side, 1), half_of(hidden_low, other, 1)
    pre_act = (
        contract(hid_mine, up_weight, 1, 0) + contract(hid_other, up_other, 1, 0) + bias_up
    )
    activ_low = gelu_exact(pre_act).astype(BF)
    act_mine, act_other = half_of(activ_low, side, 1), half_of(activ_low, other, 1)
    ffn = (
        contract(act_mine, down_weight, 1, 0) + contract(act_other, down_other, 1, 0) + bias_down
    )
    resid_two = hidden + ffn
    upstream = cotangent[0].astype(F32)
    result, norm_two_back = jax.vjp(layer_norm, resid_two, gain_two, shift_two)
    grad_two, grad_gain_two, grad_shift_two = norm_two_back(upstream)
    two_low = grad_two.astype(BF)

    def in_order(mine, others):
        return jnp.where(
            side == 0,
            jnp.concatenate([mine, others], 1),
            jnp.concatenate([others, mine], 1),
        )

    grad_activ = in_order(contract(two_low, down_weight, 1, 1), contract(two_low, down_other, 1, 1))
    gelu_back = jax.vjp(gelu_exact, pre_act)[1]
    grad_pre = gelu_back(grad_activ)[0]
    pre_low = grad_pre.astype(BF)
    grad_hidden = grad_two + in_order(
        contract(pre_low, up_weight, 1, 1), contract(pre_low, up_other, 1, 1)
    )
    norm_one_back = jax.vjp(layer_norm, resid_one, gain_one, shift_one)[1]
    grad_one, grad_gain_one, grad_shift_one = norm_one_back(grad_hidden)
    one_low = grad_one.astype(BF)
    to_out_mine = contract(out_weight, one_low, 1, 1)
    to_out_other = contract(out_other, one_low, 1, 1)
    grad_att = jnp.where(
        side == 0,
        jnp.concatenate([to_out_mine, to_out_other], 0),
        jnp.concatenate([to_out_other, to_out_mine], 0),
    ).astype(BF)
    grad_chunks = jnp.pad(
        grad_att.reshape(HEADS, HEAD_DIM, rows), ((0, slots - HEADS), (0, 0), (0, 0))
    )
    grad_heads = to_heads(grad_chunks)

    def both(mine, theirs, axis=0):
        return jnp.concatenate([mine, swap(theirs)], axis)

    grad_down = contract(both(act_mine, act_other), both(two_low, two_low), 0, 0).astype(BF)
    grad_up = contract(both(hid_mine, hid_other), both(pre_low, pre_low), 0, 0).astype(BF)
    grad_out = contract(both(att_mine, att_other, 1), both(one_low, one_low), 1, 0).astype(BF)

    backs = []
    for i in range(per):
        _, full, lse, feat_q, feat_k, val = kept[i]
        backs.append(attn_bwd(gathered[:, i], grad_heads[:, i], full, lse, feat_q, feat_k, val))
    grad_qkv_low = to_tokens(jnp.stack(backs, 1))
    grad_qkv_low = grad_qkv_low.reshape(HEADS, 3, HEAD_DIM, rows)
    grad_qkv_low = jnp.transpose(grad_qkv_low, (1, 0, 2, 3)).reshape(3 * width, rows)
    grad_qkv = contract(
        both(in_mine, in_other), both(grad_qkv_low, grad_qkv_low, 1), 0, 1
    ).astype(BF)
    grad_input = (
        grad_one
        + in_order(
            contract(grad_qkv_low, qkv_weight, 0, 1), contract(grad_qkv_low, qkv_other, 0, 1)
        )
    ).astype(BF)

    small = (
        jnp.sum(grad_qkv_low[:width].astype(F32), axis=1),
        jnp.sum(grad_qkv_low[2 * width :].astype(F32), axis=1),
        jnp.sum(grad_one, axis=0),
        jnp.sum(grad_pre, axis=0),
        jnp.sum(grad_two, axis=0),
        grad_gain_one,
        grad_shift_one,
        grad_gain_two,
        grad_shift_two,
    )
    small_halves = jnp.concatenate([item.reshape(2, -1) for item in small], 1)
    small_mine = half_of(small_halves, side, 0) + swap(half_of(small_halves, other, 0))
    small_mine = small_mine.reshape(-1, 128)
    bits = list(range(count.bit_length() - 1))
    for bit in bits:
        small_mine = small_mine + exchange(small_mine, bit, count)
    small_mine = small_mine.reshape(-1)
    first = bits
    second = [bits[1], bits[0]] + bits[2:]
    third = bits[2:] + bits[:2]
    summed = (
        sum_over_tokens(grad_qkv, (896, 896, 512), (first, second, third), count, place),
        sum_over_tokens(grad_out, (768,), (third,), count, place),
        sum_over_tokens(grad_up, (2304, 768), (second, third), count, place),
        sum_over_tokens(grad_down, (512, 256), (first, third), count, place),
    )
    return (
        result.astype(BF)[None],
        grad_input[None],
        *summed,
        *(small_mine[starts[i] : starts[i + 1]] for i in range(9)),
    )


def solution(mesh):
    matrix = P("fsdp", None)
    vector = P("fsdp")
    rows = P("fsdp", "ctx", None)
    return jax.shard_map(
        functools.partial(per_device, mesh.shape["ctx"]),
        mesh=mesh,
        in_specs=(rows, rows) + (matrix,) * 4 + (vector,) * 9 + (rows,),
        out_specs=(rows, rows) + (matrix,) * 4 + (vector,) * 9,
        check_vma=False,
    )
```
